32 devices in a mesh: groups: 2 (over y), rows: 4 (over z), cols: 4 (over x, core).
Axes of the slice: x: 2, y: 2, z: 4, core: 2. Of those that a mesh axis runs over, the one named last changes fastest.
Arguments:
- hidden: bfloat16 [64, 32, 1280], P(('groups', 'rows'), 'cols'), parts along dimension 0, may hold values from -6 to 6
- ln_gain: float32 [1280], replicated, may hold values from 0.1 to 1.9
- ln_bias: float32 [1280], replicated, may hold values from -3 to 3
- w_query: bfloat16 [1280, 256], P(None, 'cols'), may hold values from -8.944272 to 8.944272
- w_keyval: bfloat16 [1280, 512], P(None, 'cols'), may hold values from -0.3125 to 0.3125
- stale_keyval: bfloat16 [64, 32, 4, 128], P(('groups', 'rows'), None, 'cols'), parts along dimension 0, may hold values from -10 to 10
- w_out: bfloat16 [256, 1280], replicated, may hold values from -0.375 to 0.375
- out_bias: float32 [1280], replicated, may hold values from -3 to 3
Outputs:
- output_rows: bfloat16 [64, 32, 1280], P(('groups', 'rows'), 'cols'), parts along dimension 0
- fresh_keyval: bfloat16 [64, 32, 4, 128], P(('groups', 'rows'), None, 'cols'), parts along dimension 0
The draws below stay inside these ranges and needn't reach their ends.
There are 2 independent parts, one for each index of `groups`. The reference program is written for one: setup_inputs(seed, part) draws one part's arguments, and reference() takes and returns one part's arrays. A program takes and returns all parts, laid end to end along the dimension named above; an argument that names none is the same for every part. Nothing has to cross between parts.
All inputs are finite; a program needn't handle non-finite values.
Results may differ from the reference program's by a relative error of at most 0.04.
The reference program's roundings to bfloat16 on the way count: a program that leaves them out, or rounds other values in their place, can miss the bound.
Values may be sent and summed in bfloat16 or wider, within the bound.
No kernel may reach another device: no remote copies, remote signals or barrier semaphores. Data moves between devices by JAX's collectives and lax.ppermute only.
A program may use at most 64 MiB of HBM per device.

```python
import math
import jax
import jax.numpy as jnp
from jax import lax

D = 1280
HD = 64
RB = 8
HEADS = 4
H = 32
W = 32
N_ROWS = 4


def draw_w_query(key, part):
    values = jnp.clip(jax.random.normal(key, (D, HEADS * HD), jnp.float32), -4.0, 4.0) * (2.0 / math.sqrt(D))
    return values.astype(jnp.bfloat16)


def block_levels(stream_key, shape, shards, smallest, top_value):
    def one(dim, shards_of):
        heights = jax.random.uniform(jax.random.fold_in(jax.random.fold_in(stream_key, 6), dim), (shards_of,), jnp.float32, smallest / len(shards), top_value / len(shards))
        return jnp.repeat(jnp.exp(heights), shape[dim] // shards_of).reshape((-1,) + (1,) * (len(shape) - dim - 1))

    factor_of = one(*shards[0])
    for cut in shards[1:]:
        factor_of = factor_of * one(*cut)
    return factor_of


def bell_draw(own_key, shape, deviation, reach, split=(), kind=jnp.bfloat16):
    array = deviation * jax.random.normal(own_key, shape, jnp.float32)
    if split:
        array = array * block_levels(own_key, shape, split, -0.22, 0.18)
    return jnp.clip(array, -reach, reach).astype(kind)


def setup_inputs(seed: int = 0, part: int = 0) -> dict:
    seeds = jax.random.split(jax.random.key(seed), 9)
    own_keys = jax.random.split(jax.random.fold_in(seeds[8], part), 9)
    hidden = bell_draw(own_keys[0], (H, W, D), 1.0, 6.0, ((0, 4), (1, 4)))
    ln_gain = jnp.clip(1.0 + 0.18 * jax.random.normal(seeds[1], (D,), jnp.float32), 0.1, 1.9)
    ln_bias = bell_draw(seeds[2], (D,), 0.5, 3.0, (), jnp.float32)
    w_query = draw_w_query(jax.random.fold_in(seeds[8], 71), part)
    w_keyval = bell_draw(seeds[4], (D, HEADS * 2 * HD), (D // 4) ** -0.5, 0.3125, ((1, 4),))
    stale_keyval = bell_draw(own_keys[5], (H, W, HEADS, 2 * HD), 2.0, 10.0, ((0, 4), (2, 4)))
    w_out = bell_draw(seeds[6], (HEADS * HD, D), (HEADS * HD) ** -0.5, 0.375)
    out_bias = bell_draw(seeds[7], (D,), 0.5, 3.0, (), jnp.float32)
    return dict(hidden=hidden, ln_gain=ln_gain, ln_bias=ln_bias, w_query=w_query, w_keyval=w_keyval, stale_keyval=stale_keyval, w_out=w_out, out_bias=out_bias)


def layer_norm(hidden, ln_gain, ln_bias):
    values = hidden.astype(jnp.float32)
    row_mean = lax.optimization_barrier(jnp.mean(values, axis=-1, keepdims=True))
    centred = values - row_mean
    variance = lax.optimization_barrier(jnp.mean(centred * centred, axis=-1, keepdims=True))
    return (centred * lax.rsqrt(variance + 1e-05) * ln_gain + ln_bias).astype(jnp.bfloat16)

def reference(hidden, ln_gain, ln_bias, w_query, w_keyval, stale_keyval, w_out, out_bias):
    rows_all, cols_all, channels = hidden.shape
    normed = layer_norm(hidden, ln_gain, ln_bias).reshape(-1, channels)
    queries = jnp.dot(normed, w_query, preferred_element_type=jnp.float32).astype(jnp.bfloat16)
    queries = queries.reshape(rows_all, cols_all, HEADS, HD)
    keyval = jnp.dot(normed, w_keyval, preferred_element_type=jnp.float32).astype(jnp.bfloat16)
    keyval = keyval.reshape(rows_all, cols_all, HEADS, 2 * HD)
    score_scale = 1.0 / math.sqrt(HD)

    def one_task(position):
        band_index = (position // HEADS).astype(jnp.int32)
        head_index = (position % HEADS).astype(jnp.int32)
        first_row = (band_index * RB).astype(jnp.int32)
        head_queries = lax.dynamic_index_in_dim(queries, head_index, 2, keepdims=False)
        band_queries = lax.dynamic_slice_in_dim(head_queries, first_row, RB, 0).reshape(RB * cols_all, HD)
        stale_keys = lax.dynamic_index_in_dim(stale_keyval, head_index, 2, keepdims=False)
        fresh_keys = lax.dynamic_slice_in_dim(lax.dynamic_index_in_dim(keyval, head_index, 2, keepdims=False), first_row, RB, 0)
        merged = lax.dynamic_update_slice_in_dim(stale_keys, fresh_keys, first_row, 0).reshape(-1, 2 * HD)
        scores = jnp.dot(band_queries, merged[:, :HD].T, preferred_element_type=jnp.float32) * score_scale
        row_max = lax.optimization_barrier(jnp.max(scores, axis=-1, keepdims=True))
        weights = jnp.exp(scores - row_max)
        denominator = lax.optimization_barrier(jnp.sum(weights, axis=-1, keepdims=True))
        summed = jnp.dot(weights.astype(jnp.bfloat16), merged[:, HD:], preferred_element_type=jnp.float32)
        return (summed / denominator).astype(jnp.bfloat16)
    attention = lax.map(one_task, jnp.arange(N_ROWS * HEADS, dtype=jnp.int32))
    attention = attention.reshape(N_ROWS, HEADS, RB, cols_all, HD).transpose(0, 2, 3, 1, 4)
    attention = attention.reshape(rows_all * cols_all, HEADS * HD)
    projected = jnp.dot(attention, w_out, preferred_element_type=jnp.float32)
    output_rows = projected + out_bias + hidden.reshape(-1, channels).astype(jnp.float32)
    output_rows = output_rows.astype(jnp.bfloat16).reshape(rows_all, cols_all, channels)
    return (output_rows, keyval)
```

```python
import functools
import math

import jax
import jax.numpy as jnp
from jax import lax
from jax.experimental import pallas as pl
from jax.experimental.pallas import tpu as pltpu
from jax.sharding import PartitionSpec as P

SCORE_BUDGET = 1 << 17
VMEM = pl.BlockSpec(memory_space=pltpu.VMEM)
PARAMS = pltpu.CompilerParams(vmem_limit_bytes=24 << 20)
SMEM = pl.BlockSpec(memory_space=pltpu.SMEM)


def near(*arrays):
    return [pltpu.with_memory_space_constraint(a, pltpu.VMEM) for a in arrays]


def swap(block, axis, mask):
    size = lax.axis_size(axis)
    return lax.ppermute(block, axis, [(i, i ^ mask) for i in range(size)])


def gather_by_mask(block, axis):
    size = lax.axis_size(axis)
    blocks = {0: block}
    bit = size // 2
    while bit:
        for mask in sorted(blocks):
            blocks[mask | bit] = swap(blocks[mask], axis, bit)
        bit //= 2
    return [blocks[m] for m in range(size)]


def project_kernel(count, *refs):
    strips, (gain, bias, weights, q_out, kv_out) = refs[:count], refs[count:]
    rows = strips[0].shape[0]
    lanes = kv_out.shape[1]
    normed = []
    for strip in strips:
        values = strip[...].astype(jnp.float32)
        centred = values - jnp.mean(values, axis=-1, keepdims=True)
        variance = jnp.mean(centred * centred, axis=-1, keepdims=True)
        normed.append(
            (centred * lax.rsqrt(variance + 1e-05) * gain[...] + bias[...]).astype(jnp.bfloat16)
        )
    both = jnp.concatenate(normed, axis=0)
    out = jnp.dot(both, weights[...], preferred_element_type=jnp.float32).astype(jnp.bfloat16)
    q_out[...] = out[:, :lanes]
    kv_out[...] = out[:, lanes:]


def project(strips, gain, bias, weights):
    rows = len(strips) * strips[0].shape[0]
    lanes = weights.shape[1] // 2
    shape = pltpu.VMEM((rows, lanes), jnp.bfloat16)
    return pl.pallas_call(
        functools.partial(project_kernel, len(strips)),
        out_shape=(shape, shape),
        in_specs=[VMEM] * (len(strips) + 3),
        out_specs=(VMEM, VMEM),
        compiler_params=PARAMS,
        name="project",
    )(*near(*strips, gain, bias, weights))


def attend_kernel(blocks, head_size, tile, q_ref, *refs):
    key_refs, (out_ref, scores) = refs[:blocks], refs[blocks:]
    factor = math.log2(math.e) / math.sqrt(head_size)

    def one(index):
        rows = pl.ds(pl.multiple_of(index * tile, tile), tile)
        queries = q_ref[rows, :]
        start, row_max = 0, None
        for key in key_refs:
            size = key.shape[0]
            part = lax.dot_general(
                queries, key[...], (((1,), (1,)), ((), ())), preferred_element_type=jnp.float32
            )
            scores[:, start : start + size] = part
            top = jnp.max(part, axis=-1, keepdims=True)
            row_max = top if row_max is None else jnp.maximum(row_max, top)
            start += size
        start, total, weighted = 0, None, None
        for key in key_refs:
            size = key.shape[0]
            weights = jnp.exp2((scores[:, start : start + size] - row_max) * factor)
            part_sum = jnp.sum(weights, axis=-1, keepdims=True)
            part = jnp.dot(
                weights.astype(jnp.bfloat16), key[...], preferred_element_type=jnp.float32
            )
            total = part_sum if total is None else total + part_sum
            weighted = part if weighted is None else weighted + part
            start += size
        out_ref[rows, :] = (weighted[:, head_size:] / total).astype(jnp.bfloat16)

    steps = q_ref.shape[0] // tile
    if steps == 1:
        one(0)
    else:
        lax.fori_loop(0, steps, lambda index, carry: (one(index), carry)[1], 0)


def attend(queries, keys, head_size):
    rows = queries.shape[0]
    key_count = sum(k.shape[0] for k in keys)
    tile = rows
    while tile * key_count > SCORE_BUDGET and tile % 32 == 0:
        tile //= 2
    return pl.pallas_call(
        functools.partial(attend_kernel, len(keys), head_size, tile),
        out_shape=pltpu.VMEM((rows, head_size), jnp.bfloat16),
        in_specs=[VMEM] * (1 + len(keys)),
        out_specs=VMEM,
        scratch_shapes=[pltpu.VMEM((tile, key_count), jnp.float32)],
        compiler_params=PARAMS,
        name="attend",
    )(*near(queries, *keys))


def finish_kernel(count, col_ref, *refs):
    parts, (w_ref, bias, hidden, out_ref) = refs[:count], refs[count:]
    head_size = parts[0].shape[1]
    total = hidden[...].astype(jnp.float32) + bias[...]
    for mask, part in enumerate(parts):
        head = jnp.bitwise_xor(col_ref[0], mask)
        rows = w_ref[pl.ds(pl.multiple_of(head * head_size, head_size), head_size), :]
        total = total + jnp.dot(part[...], rows, preferred_element_type=jnp.float32)
    out_ref[...] = total.astype(jnp.bfloat16)


def finish(col, parts, w_out, bias, hidden):
    return pl.pallas_call(
        functools.partial(finish_kernel, len(parts)),
        out_shape=jax.ShapeDtypeStruct(hidden.shape, jnp.bfloat16),
        in_specs=[SMEM] + [VMEM] * (len(parts) + 3),
        out_specs=VMEM,
        compiler_params=PARAMS,
        name="finish",
    )(col, *near(*parts, w_out, bias, hidden))


def place_kernel(count, col_ref, *refs):
    blocks, out_ref = refs[:-1], refs[-1]
    rows, _, width, lanes = out_ref.shape
    each = rows * width
    for mask in range(count):
        strip = jnp.bitwise_xor(col_ref[0], mask)
        half, at = divmod(mask * each, blocks[0].shape[0])
        out_ref[:, strip] = blocks[half][at : at + each, :].reshape(rows, width, lanes)


def place(col, blocks, shape):
    return pl.pallas_call(
        functools.partial(place_kernel, shape[1]),
        out_shape=jax.ShapeDtypeStruct(shape, jnp.bfloat16),
        in_specs=[SMEM] + [VMEM] * len(blocks),
        out_specs=VMEM,
        compiler_params=PARAMS,
        name="place",
    )(col, *near(*blocks))


def shards(hidden, ln_gain, ln_bias, w_query, w_keyval, stale_keyval, w_out, out_bias):
    band_rows, strip_cols, channels = hidden.shape
    head_size = w_query.shape[1]
    size = lax.axis_size("cols")
    half = size // 2
    each = band_rows * strip_cols
    own = hidden.reshape(each, channels)
    col = lax.axis_index("cols").astype(jnp.int32).reshape(1)
    weights = jnp.concatenate([w_query, jnp.zeros_like(w_query), w_keyval], axis=1)
    gain, bias = ln_gain.reshape(1, -1), ln_bias.reshape(1, -1)

    stale = gather_by_mask(stale_keyval.reshape(-1, 2 * head_size), "rows")[1:]
    strips = gather_by_mask(own, "cols")
    q_home, kv_home = project(strips[:half], gain, bias, weights)
    q_away, kv_away = project(strips[half:], gain, bias, weights)
    keys = [kv_home, kv_away] + stale
    away = attend(q_away, keys, head_size)
    home = attend(q_home, keys, head_size)
    mine = {0: home[:each]}
    for mask in range(size - 1, 0, -1):
        block = away if mask >= half else home
        at = (mask % half) * each
        mine[mask] = swap(block[at : at + each], "cols", mask)
    output = finish(
        col, [mine[m] for m in range(size)], w_out, out_bias.reshape(1, -1), own
    )
    fresh = place(col, [kv_home, kv_away], (band_rows, size, strip_cols, 2 * head_size))
    return (
        output.reshape(hidden.shape),
        fresh.reshape(band_rows, size * strip_cols, 1, 2 * head_size),
    )


def solution(mesh):
    return jax.shard_map(
        shards,
        mesh=mesh,
        in_specs=(
            P(("groups", "rows"), "cols", None),
            P(),
            P(),
            P(None, "cols"),
            P(None, "cols"),
            P(("groups", "rows"), None, "cols", None),
            P(),
            P(),
        ),
        out_specs=(P(("groups", "rows"), "cols", None), P(("groups", "rows"), None, "cols", None)),
        check_vma=False,
    )
```

```python
import functools
import math

import jax
import jax.numpy as jnp
from jax import lax
from jax.experimental import pallas as pl
from jax.experimental.pallas import tpu as pltpu
from jax.sharding import PartitionSpec as P


SCORE_BUDGET = 1 << 17
VMEM = pl.BlockSpec(memory_space=pltpu.VMEM)
PARAMS = pltpu.CompilerParams(vmem_limit_bytes=24 << 20)
HBM = pl.BlockSpec(memory_space=pltpu.HBM)
SMEM = pl.BlockSpec(memory_space=pltpu.SMEM)


def near(*arrays):
    return [pltpu.with_memory_space_constraint(a, pltpu.VMEM) for a in arrays]


def swap(block, axis, mask):
    size = lax.axis_size(axis)
    return lax.ppermute(block, axis, [(i, i ^ mask) for i in range(size)])


def gather_plan(size):
    plan = []
    for mask in range(1, size):
        low = mask & -mask
        plan.append((mask, mask - low, low))
    return sorted(plan, key=lambda step: (bin(step[0]).count("1"), -step[2]))


def gather_bands(block, axis):
    return [block] + [swap(block, axis, m) for m in range(1, lax.axis_size(axis))]


def gather_by_mask(block, axis):
    size = lax.axis_size(axis)
    blocks = {0: block}
    for mask, source, bit in gather_plan(size):
        blocks[mask] = swap(blocks[source], axis, bit)
    return [blocks[m] for m in range(size)]


def project_rows(strips, gain, bias, w_query, w_keyval, q_out, kv_out):
    scale, shift = gain[...].reshape(1, -1), bias[...].reshape(1, -1)
    normed = []
    for strip in strips:
        values = strip[...].astype(jnp.float32)
        centred = values - jnp.mean(values, axis=-1, keepdims=True)
        variance = jnp.mean(centred * centred, axis=-1, keepdims=True)
        normed.append(
            (centred * lax.rsqrt(variance + 1e-05) * scale + shift).astype(jnp.bfloat16)
        )
    both = jnp.concatenate(normed, axis=0)
    queries = lax.dot_general(
        both, w_query[...], (((1,), (1,)), ((), ())), preferred_element_type=jnp.float32
    ).astype(jnp.bfloat16)
    q_out[...] = jnp.concatenate([queries, jnp.zeros_like(queries)], axis=1)
    kv_out[...] = jnp.dot(both, w_keyval[...], preferred_element_type=jnp.float32).astype(
        jnp.bfloat16
    )


def load_kernel(count, *refs):
    sources, targets, arrived = refs[:count], refs[count:-1], refs[-1]
    copies = [
        pltpu.make_async_copy(source, target, arrived.at[i])
        for i, (source, target) in enumerate(zip(sources, targets))
    ]
    for copy in copies:
        copy.start()
    for copy in copies:
        copy.wait()


def load(*arrays):
    count = len(arrays)
    return pl.pallas_call(
        functools.partial(load_kernel, count),
        out_shape=tuple(pltpu.VMEM(a.shape, a.dtype) for a in arrays),
        in_specs=[HBM] * count,
        out_specs=(VMEM,) * count,
        scratch_shapes=[pltpu.SemaphoreType.DMA((count,))],
        compiler_params=PARAMS,
        name="load",
    )(*(pltpu.with_memory_space_constraint(a, pltpu.HBM) for a in arrays))


def project_kernel(count, *refs):
    project_rows(refs[:count], *refs[count:])


def project(strips, *params):
    rows = len(strips) * strips[0].shape[0]
    shape = pltpu.VMEM((rows, params[-1].shape[1]), jnp.bfloat16)
    return pl.pallas_call(
        functools.partial(project_kernel, len(strips)),
        out_shape=(shape, shape),
        in_specs=[VMEM] * (len(strips) + len(params)),
        out_specs=(VMEM, VMEM),
        compiler_params=PARAMS,
        name="project",
    )(*near(*strips, *params))


def attend_kernel(blocks, head_size, tile, q_ref, *refs):
    key_refs, (out_ref, scores) = refs[:blocks], refs[blocks:]
    factor = math.log2(math.e) / math.sqrt(head_size)

    def one(index):
        rows = pl.ds(pl.multiple_of(index * tile, tile), tile)
        queries = q_ref[rows, :]
        start, row_max = 0, None
        for key in key_refs:
            size = key.shape[0]
            part = lax.dot_general(
                queries, key[...], (((1,), (1,)), ((), ())), preferred_element_type=jnp.float32
            )
            scores[:, start : start + size] = part
            top = jnp.max(part, axis=-1, keepdims=True)
            row_max = top if row_max is None else jnp.maximum(row_max, top)
            start += size
        start, total, weighted = 0, None, None
        for key in key_refs:
            size = key.shape[0]
            weights = jnp.exp2((scores[:, start : start + size] - row_max) * factor)
            part_sum = jnp.sum(weights, axis=-1, keepdims=True)
            part = jnp.dot(
                weights.astype(jnp.bfloat16), key[...], preferred_element_type=jnp.float32
            )
            total = part_sum if total is None else total + part_sum
            weighted = part if weighted is None else weighted + part
            start += size
        out_ref[rows, :] = (weighted[:, head_size:] / total).astype(jnp.bfloat16)

    steps = q_ref.shape[0] // tile
    if steps == 1:
        one(0)
    else:
        lax.fori_loop(0, steps, lambda index, carry: (one(index), carry)[1], 0)


def attend(queries, keys, head_size):
    rows = queries.shape[0]
    key_count = sum(k.shape[0] for k in keys)
    tile = rows
    while tile * key_count > SCORE_BUDGET and tile % 32 == 0:
        tile //= 2
    return pl.pallas_call(
        functools.partial(attend_kernel, len(keys), head_size, tile),
        out_shape=pltpu.VMEM((rows, head_size), jnp.bfloat16),
        in_specs=[VMEM] * (1 + len(keys)),
        out_specs=VMEM,
        scratch_shapes=[pltpu.VMEM((tile, key_count), jnp.float32)],
        compiler_params=PARAMS,
        name="attend",
    )(*near(queries, *keys))


def head_rows(col_ref, mask, w_ref, head_size):
    head = jnp.bitwise_xor(col_ref[0], mask)
    return w_ref[pl.ds(pl.multiple_of(head * head_size, head_size), head_size), :]


def place_kernel(each, col_ref, *refs):
    *blocks, own, w_ref, bias, hidden, fresh_out, base_out, fresh, sent = refs
    rows, count, width, lanes = fresh.shape
    for mask in range(count):
        strip = jnp.bitwise_xor(col_ref[0], mask)
        half, at = divmod(mask * each, blocks[0].shape[0])
        fresh[:, strip] = blocks[half][at : at + each, :].reshape(rows, width, lanes)
    copy = pltpu.make_async_copy(fresh, fresh_out, sent)
    copy.start()
    product = jnp.dot(
        own[...], head_rows(col_ref, 0, w_ref, own.shape[1]), preferred_element_type=jnp.float32
    )
    base_out[...] = product + bias[...] + hidden[...].astype(jnp.float32)
    copy.wait()


def place(col, blocks, own, w_out, bias, hidden, shape):
    return pl.pallas_call(
        functools.partial(place_kernel, own.shape[0]),
        out_shape=(
            jax.ShapeDtypeStruct(shape, jnp.bfloat16),
            pltpu.VMEM(hidden.shape, jnp.float32),
        ),
        in_specs=[SMEM] + [VMEM] * (len(blocks) + 4),
        out_specs=(HBM, VMEM),
        scratch_shapes=[pltpu.VMEM(shape, jnp.bfloat16), pltpu.SemaphoreType.DMA],
        compiler_params=PARAMS,
        name="place",
    )(col, *near(*blocks, own, w_out, bias, hidden))


def finish_kernel(col_ref, base, *refs):
    *parts, w_ref, out_ref, ready, sent = refs
    head_size = parts[0].shape[1]
    rows = [head_rows(col_ref, mask, w_ref, head_size) for mask in range(1, len(parts) + 1)]
    values = [part[...] for part in parts]
    channels = base.shape[1]
    step = channels // 2 if channels % 256 == 0 else channels
    copies = []
    for index, start in enumerate(range(0, channels, step)):
        columns = slice(start, start + step)
        total = base[:, columns]
        for value, row in zip(values, rows):
            total = total + jnp.dot(
                value, row[:, columns], preferred_element_type=jnp.float32
            )
        ready[:, columns] = total.astype(jnp.bfloat16)
        copy = pltpu.make_async_copy(ready.at[:, columns], out_ref.at[:, columns], sent.at[index])
        copy.start()
        copies.append(copy)
    for copy in copies:
        copy.wait()


def finish(col, base, parts, w_out):
    return pl.pallas_call(
        finish_kernel,
        out_shape=jax.ShapeDtypeStruct(base.shape, jnp.bfloat16),
        in_specs=[SMEM] + [VMEM] * (len(parts) + 2),
        out_specs=HBM,
        scratch_shapes=[pltpu.VMEM(base.shape, jnp.bfloat16), pltpu.SemaphoreType.DMA((2,))],
        compiler_params=PARAMS,
        name="finish",
    )(col, *near(base, *parts, w_out))


def shards(hidden, ln_gain, ln_bias, w_query, w_keyval, stale_keyval, w_out, out_bias):
    band_rows, strip_cols, channels = hidden.shape
    head_size = w_query.shape[1]
    size = lax.axis_size("cols")
    half = size // 2
    each = band_rows * strip_cols
    own = hidden.reshape(each, channels)
    col = lax.axis_index("cols").astype(jnp.int32).reshape(1)
    strips = gather_by_mask(own, "cols")
    stale = gather_bands(stale_keyval.reshape(-1, 2 * head_size), "rows")[1:]
    near_own, *params = load(own, ln_gain, ln_bias, w_query.T, w_keyval)
    q_home, kv_home = project([near_own, *strips[1:half]], *params)
    q_away, kv_away = project(strips[half:], *params)
    keys = [kv_home, kv_away] + stale
    away = attend(q_away, keys, head_size)
    home = attend(q_home, keys, head_size)
    mine = {0: home[:each]}
    for mask in range(size - 1, 0, -1):
        block = away if mask >= half else home
        at = (mask % half) * each
        mine[mask] = swap(block[at : at + each], "cols", mask)
    fresh, base = place(
        col,
        [kv_home, kv_away],
        mine[0],
        w_out,
        out_bias.reshape(1, -1),
        near_own,
        (band_rows, size, strip_cols, 2 * head_size),
    )
    output = finish(col, base, [mine[m] for m in range(1, size)], w_out)
    return (
        output.reshape(hidden.shape),
        fresh.reshape(band_rows, size * strip_cols, 1, 2 * head_size),
    )


def solution(mesh):
    return jax.shard_map(
        shards,
        mesh=mesh,
        in_specs=(
            P(("groups", "rows"), "cols", None),
            P(),
            P(),
            P(None, "cols"),
            P(None, "cols"),
            P(("groups", "rows"), None, "cols", None),
            P(),
            P(),
        ),
        out_specs=(P(("groups", "rows"), "cols", None), P(("groups", "rows"), None, "cols", None)),
        check_vma=False,
    )
```

```python
import functools
import math

import jax
import jax.numpy as jnp
from jax import lax
from jax.experimental import pallas as pl
from jax.experimental.pallas import tpu as pltpu
from jax.sharding import PartitionSpec as P


SCORE_BUDGET = 1 << 17
VMEM = pl.BlockSpec(memory_space=pltpu.VMEM)
PARAMS = pltpu.CompilerParams(vmem_limit_bytes=24 << 20)
HBM = pl.BlockSpec(memory_space=pltpu.HBM)
SMEM = pl.BlockSpec(memory_space=pltpu.SMEM)


def near(*arrays):
    return [pltpu.with_memory_space_constraint(a, pltpu.VMEM) for a in arrays]


def swap(block, axis, mask):
    size = lax.axis_size(axis)
    return lax.ppermute(block, axis, [(i, i ^ mask) for i in range(size)])


def gather_plan(size):
    plan = []
    for mask in range(1, size):
        low = mask & -mask
        plan.append((mask, mask - low, low))
    return sorted(plan, key=lambda step: (bin(step[0]).count("1"), -step[2]))


def gather_bands(block, axis):
    size = lax.axis_size(axis)
    blocks = []
    for step in range(1, size):
        blocks.append(lax.ppermute(block, axis, [(i, (i + step) % size) for i in range(size)]))
    return blocks


def gather_by_mask(block, axis):
    size = lax.axis_size(axis)
    blocks = {0: block}
    for mask, source, bit in gather_plan(size):
        blocks[mask] = swap(blocks[source], axis, bit)
    return [blocks[m] for m in range(size)]


def project_rows(strips, gain, bias, w_query, w_keyval, q_out, kv_out):
    scale, shift = gain[...].reshape(1, -1), bias[...].reshape(1, -1)
    normed = []
    for strip in strips:
        values = strip[...].astype(jnp.float32)
        centred = values - jnp.mean(values, axis=-1, keepdims=True)
        variance = jnp.mean(centred * centred, axis=-1, keepdims=True)
        normed.append(
            (centred * lax.rsqrt(variance + 1e-05) * scale + shift).astype(jnp.bfloat16)
        )
    both = jnp.concatenate(normed, axis=0)
    queries = lax.dot_general(
        both, w_query[...], (((1,), (1,)), ((), ())), preferred_element_type=jnp.float32
    ).astype(jnp.bfloat16)
    q_out[...] = jnp.concatenate([queries, jnp.zeros_like(queries)], axis=1)
    kv_out[...] = jnp.dot(both, w_keyval[...], preferred_element_type=jnp.float32).astype(
        jnp.bfloat16
    )


def load_kernel(count, *refs):
    sources, targets, arrived = refs[:count], refs[count:-1], refs[-1]
    copies = [
        pltpu.make_async_copy(source, target, arrived.at[i])
        for i, (source, target) in enumerate(zip(sources, targets))
    ]
    for copy in copies:
        copy.start()
    for copy in copies:
        copy.wait()


def load(*arrays):
    count = len(arrays)
    return pl.pallas_call(
        functools.partial(load_kernel, count),
        out_shape=tuple(pltpu.VMEM(a.shape, a.dtype) for a in arrays),
        in_specs=[HBM] * count,
        out_specs=(VMEM,) * count,
        scratch_shapes=[pltpu.SemaphoreType.DMA((count,))],
        compiler_params=PARAMS,
        name="load",
    )(*(pltpu.with_memory_space_constraint(a, pltpu.HBM) for a in arrays))


def project_kernel(count, *refs):
    project_rows(refs[:count], *refs[count:])


def project(strips, *params):
    rows = len(strips) * strips[0].shape[0]
    shape = pltpu.VMEM((rows, params[-1].shape[1]), jnp.bfloat16)
    return pl.pallas_call(
        functools.partial(project_kernel, len(strips)),
        out_shape=(shape, shape),
        in_specs=[VMEM] * (len(strips) + len(params)),
        out_specs=(VMEM, VMEM),
        compiler_params=PARAMS,
        name="project",
    )(*near(*strips, *params))


def attend_rows(head_size, tile, q_ref, key_refs, out_ref, scores):
    factor = math.log2(math.e) / math.sqrt(head_size)

    def one(rows):
        queries = q_ref[rows, :]
        start, row_max = 0, None
        for key in key_refs:
            size = key.shape[0]
            part = lax.dot_general(
                queries, key[...], (((1,), (1,)), ((), ())), preferred_element_type=jnp.float32
            )
            scores[:, start : start + size] = part
            top = jnp.max(part, axis=-1, keepdims=True)
            row_max = top if row_max is None else jnp.maximum(row_max, top)
            start += size
        start, total, weighted = 0, None, None
        for key in key_refs:
            size = key.shape[0]
            weights = jnp.exp2((scores[:, start : start + size] - row_max) * factor)
            part_sum = jnp.sum(weights, axis=-1, keepdims=True)
            part = jnp.dot(
                weights.astype(jnp.bfloat16), key[...], preferred_element_type=jnp.float32
            )
            total = part_sum if total is None else total + part_sum
            weighted = part if weighted is None else weighted + part
            start += size
        out_ref[rows, :] = (weighted[:, head_size:] / total).astype(jnp.bfloat16)

    steps = q_ref.shape[0] // tile
    if steps == 1:
        one(pl.ds(0, tile))
    else:

        def step(index, carry):
            one(pl.ds(pl.multiple_of(index * tile, tile), tile))
            return carry

        lax.fori_loop(0, steps, step, 0)


def score_tile(rows, keys):
    key_count = sum(k.shape[0] for k in keys)
    tile = rows
    while tile * key_count > SCORE_BUDGET and tile % 32 == 0:
        tile //= 2
    return tile, pltpu.VMEM((tile, key_count), jnp.float32)


def away_kernel(blocks, head_size, tile, q_ref, *refs):
    attend_rows(head_size, tile, q_ref, refs[:blocks], *refs[blocks:])


def attend_away(queries, keys, head_size):
    rows = queries.shape[0]
    tile, scores = score_tile(rows, keys)
    return pl.pallas_call(
        functools.partial(away_kernel, len(keys), head_size, tile),
        out_shape=pltpu.VMEM((rows, head_size), jnp.bfloat16),
        in_specs=[VMEM] * (1 + len(keys)),
        out_specs=VMEM,
        scratch_shapes=[scores],
        compiler_params=PARAMS,
        name="attend_away",
    )(*near(queries, *keys))


def home_kernel(blocks, head_size, tile, col_ref, q_ref, *refs):
    keys, (out_ref, fresh_out, scores, fresh, sent) = refs[:blocks], refs[blocks:]
    rows, count, width, lanes = fresh.shape
    each = rows * width
    for mask in range(count):
        strip = jnp.bitwise_xor(col_ref[0], mask)
        half, at = divmod(mask * each, keys[0].shape[0])
        fresh[:, strip] = keys[half][at : at + each, :].reshape(rows, width, lanes)
    copy = pltpu.make_async_copy(fresh, fresh_out, sent)
    copy.start()

    @pl.when(col_ref[0] >= 0)
    def _():
        attend_rows(head_size, tile, q_ref, keys, out_ref, scores)

    copy.wait()


def attend_home(col, queries, keys, head_size, fresh_shape):
    rows = queries.shape[0]
    tile, scores = score_tile(rows, keys)
    return pl.pallas_call(
        functools.partial(home_kernel, len(keys), head_size, tile),
        out_shape=(
            pltpu.VMEM((rows, head_size), jnp.bfloat16),
            jax.ShapeDtypeStruct(fresh_shape, jnp.bfloat16),
        ),
        in_specs=[SMEM] + [VMEM] * (1 + len(keys)),
        out_specs=(VMEM, HBM),
        scratch_shapes=[
            scores,
            pltpu.VMEM(fresh_shape, jnp.bfloat16),
            pltpu.SemaphoreType.DMA,
        ],
        compiler_params=PARAMS,
        name="attend_home",
    )(col, *near(queries, *keys))


def head_rows(col_ref, mask, w_ref, head_size):
    head = jnp.bitwise_xor(col_ref[0], mask)
    return w_ref[pl.ds(pl.multiple_of(head * head_size, head_size), head_size), :]


def begin_kernel(col_ref, home, w_ref, bias, hidden, out_ref):
    own = home[: hidden.shape[0], :]
    product = jnp.dot(
        own, head_rows(col_ref, 0, w_ref, own.shape[1]), preferred_element_type=jnp.float32
    )
    out_ref[...] = product + bias[...].reshape(1, -1) + hidden[...].astype(jnp.float32)


def begin(col, home, w_out, bias, hidden):
    return pl.pallas_call(
        begin_kernel,
        out_shape=pltpu.VMEM(hidden.shape, jnp.float32),
        in_specs=[SMEM] + [VMEM] * 4,
        out_specs=VMEM,
        compiler_params=PARAMS,
        name="begin",
    )(col, *near(home, w_out, bias, hidden))


def finish_kernel(col_ref, base, *refs):
    *parts, w_ref, out_ref, ready, sent = refs
    head_size = parts[0].shape[1]
    rows = [head_rows(col_ref, mask, w_ref, head_size) for mask in range(1, len(parts) + 1)]
    values = [part[...] for part in parts]
    channels = base.shape[1]
    step = channels // 2 if channels % 256 == 0 else channels
    copies = []
    for index, start in enumerate(range(0, channels, step)):
        columns = slice(start, start + step)
        total = base[:, columns]
        for value, row in zip(values, rows):
            total = total + jnp.dot(
                value, row[:, columns], preferred_element_type=jnp.float32
            )
        ready[:, columns] = total.astype(jnp.bfloat16)
        copy = pltpu.make_async_copy(ready.at[:, columns], out_ref.at[:, columns], sent.at[index])
        copy.start()
        copies.append(copy)
    for copy in copies:
        copy.wait()


def finish(col, base, parts, w_out):
    return pl.pallas_call(
        finish_kernel,
        out_shape=jax.ShapeDtypeStruct(base.shape, jnp.bfloat16),
        in_specs=[SMEM] + [VMEM] * (len(parts) + 2),
        out_specs=HBM,
        scratch_shapes=[pltpu.VMEM(base.shape, jnp.bfloat16), pltpu.SemaphoreType.DMA((2,))],
        compiler_params=PARAMS,
        name="finish",
    )(col, *near(base, *parts, w_out))


def shards(hidden, ln_gain, ln_bias, w_query, w_keyval, stale_keyval, w_out, out_bias):
    band_rows, strip_cols, channels = hidden.shape
    head_size = w_query.shape[1]
    size = lax.axis_size("cols")
    half = size // 2
    each = band_rows * strip_cols
    own = hidden.reshape(each, channels)
    col = lax.axis_index("cols").astype(jnp.int32).reshape(1)
    strips = gather_by_mask(own, "cols")
    stale = gather_bands(stale_keyval.reshape(-1, 2 * head_size), "rows")
    near_own, near_out, near_bias, *params = load(
        own, w_out, out_bias, ln_gain, ln_bias, w_query.T, w_keyval
    )
    q_home, kv_home = project([near_own, *strips[1:half]], *params)
    q_away, kv_away = project(strips[half:], *params)
    keys = [kv_home, kv_away] + stale
    away = attend_away(q_away, keys, head_size)
    fresh_shape = (band_rows, size, strip_cols, 2 * head_size)
    home, fresh = attend_home(col, q_home, keys, head_size, fresh_shape)
    mine = {}
    for mask in range(size - 1, 0, -1):
        block = away if mask >= half else home
        at = (mask % half) * each
        mine[mask] = swap(block[at : at + each], "cols", mask)
    base = begin(col, home, near_out, near_bias, near_own)
    output = finish(col, base, [mine[m] for m in range(1, size)], near_out)
    return (
        output.reshape(hidden.shape),
        fresh.reshape(band_rows, size * strip_cols, 1, 2 * head_size),
    )


def solution(mesh):
    return jax.shard_map(
        shards,
        mesh=mesh,
        in_specs=(
            P(("groups", "rows"), "cols", None),
            P(),
            P(),
            P(None, "cols"),
            P(None, "cols"),
            P(("groups", "rows"), None, "cols", None),
            P(),
            P(),
        ),
        out_specs=(P(("groups", "rows"), "cols", None), P(("groups", "rows"), None, "cols", None)),
        check_vma=False,
    )
```

```python
import functools
import math

import jax
import jax.numpy as jnp
from jax import lax
from jax.experimental import pallas as pl
from jax.experimental.pallas import tpu as pltpu
from jax.sharding import PartitionSpec as P


SCORE_BUDGET = 1 << 17
VMEM = pl.BlockSpec(memory_space=pltpu.VMEM)
PARAMS = pltpu.CompilerParams(vmem_limit_bytes=24 << 20)
HBM = pl.BlockSpec(memory_space=pltpu.HBM)
SMEM = pl.BlockSpec(memory_space=pltpu.SMEM)


def near(*arrays):
    return [pltpu.with_memory_space_constraint(a, pltpu.VMEM) for a in arrays]


def swap(block, axis, mask):
    size = lax.axis_size(axis)
    return lax.ppermute(block, axis, [(i, i ^ mask) for i in range(size)])


def gather_plan(size):
    plan = []
    for mask in range(1, size):
        low = mask & -mask
        plan.append((mask, mask - low, low))
    return sorted(plan, key=lambda step: (bin(step[0]).count("1"), -step[2]))


def folded_ring(size):
    return [0, *range(1, size, 2), *reversed(range(2, size, 2))]


def gather_bands(block, axis):
    size = lax.axis_size(axis)
    ring = folded_ring(size)
    blocks = []
    for step in range(1, size):
        pairs = [(ring[i], ring[(i + step) % size]) for i in range(size)]
        blocks.append(lax.ppermute(block, axis, pairs))
    return blocks


def gather_by_mask(block, axis):
    size = lax.axis_size(axis)
    blocks = {0: block}
    for mask, source, bit in gather_plan(size):
        blocks[mask] = swap(blocks[source], axis, bit)
    return [blocks[m] for m in range(size)]


def project_rows(strips, gain, bias, w_query, w_keyval, q_out, kv_out):
    scale, shift = gain[...].reshape(1, -1), bias[...].reshape(1, -1)
    normed = []
    for strip in strips:
        values = strip[...].astype(jnp.float32)
        centred = values - jnp.mean(values, axis=-1, keepdims=True)
        variance = jnp.mean(centred * centred, axis=-1, keepdims=True)
        normed.append(
            (centred * lax.rsqrt(variance + 1e-05) * scale + shift).astype(jnp.bfloat16)
        )
    both = jnp.concatenate(normed, axis=0)
    queries = lax.dot_general(
        both, w_query[...], (((1,), (1,)), ((), ())), preferred_element_type=jnp.float32
    ).astype(jnp.bfloat16)
    q_out[...] = jnp.concatenate([queries, jnp.zeros_like(queries)], axis=1)
    kv_out[...] = jnp.dot(both, w_keyval[...], preferred_element_type=jnp.float32).astype(
        jnp.bfloat16
    )


def load_kernel(count, *refs):
    sources, targets, arrived = refs[:count], refs[count:-1], refs[-1]
    copies = [
        pltpu.make_async_copy(source, target, arrived.at[i])
        for i, (source, target) in enumerate(zip(sources, targets))
    ]
    for copy in copies:
        copy.start()
    for copy in copies:
        copy.wait()


def load(*arrays):
    count = len(arrays)
    return pl.pallas_call(
        functools.partial(load_kernel, count),
        out_shape=tuple(pltpu.VMEM(a.shape, a.dtype) for a in arrays),
        in_specs=[HBM] * count,
        out_specs=(VMEM,) * count,
        scratch_shapes=[pltpu.SemaphoreType.DMA((count,))],
        compiler_params=PARAMS,
        name="load",
    )(*(pltpu.with_memory_space_constraint(a, pltpu.HBM) for a in arrays))


def project_kernel(count, *refs):
    project_rows(refs[:count], *refs[count:])


def project(strips, *params):
    rows = len(strips) * strips[0].shape[0]
    shape = pltpu.VMEM((rows, params[-1].shape[1]), jnp.bfloat16)
    return pl.pallas_call(
        functools.partial(project_kernel, len(strips)),
        out_shape=(shape, shape),
        in_specs=[VMEM] * (len(strips) + len(params)),
        out_specs=(VMEM, VMEM),
        compiler_params=PARAMS,
        name="project",
    )(*near(*strips, *params))


def attend_rows(head_size, tile, q_ref, key_refs, out_ref, scores):
    factor = math.log2(math.e) / math.sqrt(head_size)

    def one(rows):
        queries = q_ref[rows, :]
        start, row_max = 0, None
        for key in key_refs:
            size = key.shape[0]
            part = lax.dot_general(
                queries, key[...], (((1,), (1,)), ((), ())), preferred_element_type=jnp.float32
            )
            scores[:, start : start + size] = part
            top = jnp.max(part, axis=-1, keepdims=True)
            row_max = top if row_max is None else jnp.maximum(row_max, top)
            start += size
        start, total, weighted = 0, None, None
        for key in key_refs:
            size = key.shape[0]
            weights = jnp.exp2((scores[:, start : start + size] - row_max) * factor)
            part_sum = jnp.sum(weights, axis=-1, keepdims=True)
            part = jnp.dot(
                weights.astype(jnp.bfloat16), key[...], preferred_element_type=jnp.float32
            )
            total = part_sum if total is None else total + part_sum
            weighted = part if weighted is None else weighted + part
            start += size
        out_ref[rows, :] = (weighted[:, head_size:] / total).astype(jnp.bfloat16)

    steps = q_ref.shape[0] // tile
    if steps == 1:
        one(pl.ds(0, tile))
    else:

        def step(index, carry):
            one(pl.ds(pl.multiple_of(index * tile, tile), tile))
            return carry

        lax.fori_loop(0, steps, step, 0)


def score_tile(rows, keys):
    key_count = sum(k.shape[0] for k in keys)
    tile = rows
    while tile * key_count > SCORE_BUDGET and tile % 32 == 0:
        tile //= 2
    return tile, pltpu.VMEM((tile, key_count), jnp.float32)


def away_kernel(blocks, head_size, tile, q_ref, *refs):
    attend_rows(head_size, tile, q_ref, refs[:blocks], *refs[blocks:])


def attend_away(queries, keys, head_size):
    rows = queries.shape[0]
    tile, scores = score_tile(rows, keys)
    return pl.pallas_call(
        functools.partial(away_kernel, len(keys), head_size, tile),
        out_shape=pltpu.VMEM((rows, head_size), jnp.bfloat16),
        in_specs=[VMEM] * (1 + len(keys)),
        out_specs=VMEM,
        scratch_shapes=[scores],
        compiler_params=PARAMS,
        name="attend_away",
    )(*near(queries, *keys))


def home_kernel(blocks, head_size, tile, col_ref, q_ref, *refs):
    keys, (out_ref, fresh_out, scores, fresh, sent) = refs[:blocks], refs[blocks:]
    rows, count, width, lanes = fresh.shape
    each = rows * width
    for mask in range(count):
        strip = jnp.bitwise_xor(col_ref[0], mask)
        half, at = divmod(mask * each, keys[0].shape[0])
        fresh[:, strip] = keys[half][at : at + each, :].reshape(rows, width, lanes)
    copy = pltpu.make_async_copy(fresh, fresh_out, sent)
    copy.start()

    @pl.when(col_ref[0] >= 0)
    def _():
        attend_rows(head_size, tile, q_ref, keys, out_ref, scores)

    copy.wait()


def attend_home(col, queries, keys, head_size, fresh_shape):
    rows = queries.shape[0]
    tile, scores = score_tile(rows, keys)
    return pl.pallas_call(
        functools.partial(home_kernel, len(keys), head_size, tile),
        out_shape=(
            pltpu.VMEM((rows, head_size), jnp.bfloat16),
            jax.ShapeDtypeStruct(fresh_shape, jnp.bfloat16),
        ),
        in_specs=[SMEM] + [VMEM] * (1 + len(keys)),
        out_specs=(VMEM, HBM),
        scratch_shapes=[
            scores,
            pltpu.VMEM(fresh_shape, jnp.bfloat16),
            pltpu.SemaphoreType.DMA,
        ],
        compiler_params=PARAMS,
        name="attend_home",
    )(col, *near(queries, *keys))


def head_rows(col_ref, mask, w_ref, head_size):
    head = jnp.bitwise_xor(col_ref[0], mask)
    return w_ref[pl.ds(pl.multiple_of(head * head_size, head_size), head_size), :]


def begin_kernel(masks, col_ref, home, *refs):
    *parts, w_ref, bias, hidden, out_ref = refs
    head_size = home.shape[1]
    total = bias[...].reshape(1, -1) + hidden[...].astype(jnp.float32)
    for mask, part in zip((0, *masks), (home[: hidden.shape[0], :], *(p[...] for p in parts))):
        total = total + jnp.dot(
            part, head_rows(col_ref, mask, w_ref, head_size), preferred_element_type=jnp.float32
        )
    out_ref[...] = total


def begin(col, home, parts, w_out, bias, hidden):
    return pl.pallas_call(
        functools.partial(begin_kernel, tuple(parts)),
        out_shape=pltpu.VMEM(hidden.shape, jnp.float32),
        in_specs=[SMEM] + [VMEM] * (4 + len(parts)),
        out_specs=VMEM,
        compiler_params=PARAMS,
        name="begin",
    )(col, *near(home, *parts.values(), w_out, bias, hidden))


def finish_kernel(mask, col_ref, base, part, w_ref, out_ref, ready, sent):
    rows = head_rows(col_ref, mask, w_ref, part.shape[1])
    values = part[...]
    channels = base.shape[1]
    step = channels // 2 if channels % 256 == 0 else channels
    copies = []
    for index, start in enumerate(range(0, channels, step)):
        columns = slice(start, start + step)
        product = jnp.dot(values, rows[:, columns], preferred_element_type=jnp.float32)
        ready[:, columns] = (base[:, columns] + product).astype(jnp.bfloat16)
        copy = pltpu.make_async_copy(ready.at[:, columns], out_ref.at[:, columns], sent.at[index])
        copy.start()
        copies.append(copy)
    for copy in copies:
        copy.wait()


def finish(col, base, mask, part, w_out):
    return pl.pallas_call(
        functools.partial(finish_kernel, mask),
        out_shape=jax.ShapeDtypeStruct(base.shape, jnp.bfloat16),
        in_specs=[SMEM] + [VMEM] * 3,
        out_specs=HBM,
        scratch_shapes=[pltpu.VMEM(base.shape, jnp.bfloat16), pltpu.SemaphoreType.DMA((2,))],
        compiler_params=PARAMS,
        name="finish",
    )(col, *near(base, part, w_out))


def shards(hidden, ln_gain, ln_bias, w_query, w_keyval, stale_keyval, w_out, out_bias):
    band_rows, strip_cols, channels = hidden.shape
    head_size = w_query.shape[1]
    size = lax.axis_size("cols")
    half = size // 2
    each = band_rows * strip_cols
    own = hidden.reshape(each, channels)
    col = lax.axis_index("cols").astype(jnp.int32).reshape(1)
    strips = gather_by_mask(own, "cols")
    stale = gather_bands(stale_keyval.reshape(-1, 2 * head_size), "rows")
    near_own, near_out, near_bias, *params = load(
        own, w_out, out_bias, ln_gain, ln_bias, w_query.T, w_keyval
    )
    q_home, kv_home = project([near_own, *strips[1:half]], *params)
    q_away, kv_away = project(strips[half:], *params)
    keys = [kv_home, kv_away] + stale
    away = attend_away(q_away, keys, head_size)
    fresh_shape = (band_rows, size, strip_cols, 2 * head_size)
    home, fresh = attend_home(col, q_home, keys, head_size, fresh_shape)
    mine = {}
    for mask in range(size - 1, 0, -1):
        block = away if mask >= half else home
        at = (mask % half) * each
        mine[mask] = swap(block[at : at + each], "cols", mask)
    last = mine.pop(half)
    base = begin(col, home, mine, near_out, near_bias, near_own)
    output = finish(col, base, half, last, near_out)
    return (
        output.reshape(hidden.shape),
        fresh.reshape(band_rows, size * strip_cols, 1, 2 * head_size),
    )


def solution(mesh):
    return jax.shard_map(
        shards,
        mesh=mesh,
        in_specs=(
            P(("groups", "rows"), "cols", None),
            P(),
            P(),
            P(None, "cols"),
            P(None, "cols"),
            P(("groups", "rows"), None, "cols", None),
            P(),
            P(),
        ),
        out_specs=(P(("groups", "rows"), "cols", None), P(("groups", "rows"), None, "cols", None)),
        check_vma=False,
    )
```

```python
import functools
import math

import jax
import jax.numpy as jnp
from jax import lax
from jax.experimental import pallas as pl
from jax.experimental.pallas import tpu as pltpu
from jax.sharding import PartitionSpec as P


SCORE_BUDGET = 1 << 17
VMEM = pl.BlockSpec(memory_space=pltpu.VMEM)
PARAMS = pltpu.CompilerParams(vmem_limit_bytes=24 << 20)
HBM = pl.BlockSpec(memory_space=pltpu.HBM)
SMEM = pl.BlockSpec(memory_space=pltpu.SMEM)


def near(*arrays):
    return [pltpu.with_memory_space_constraint(a, pltpu.VMEM) for a in arrays]


def swap(block, axis, mask):
    size = lax.axis_size(axis)
    return lax.ppermute(block, axis, [(i, i ^ mask) for i in range(size)])


def gather_plan(size):
    plan = []
    for mask in range(1, size):
        low = mask & -mask
        plan.append((mask, mask - low, low))
    return sorted(plan, key=lambda step: (bin(step[0]).count("1"), -step[2]))


def folded_ring(size):
    return [0, *range(1, size, 2), *reversed(range(2, size, 2))]


def gather_bands(block, axis):
    size = lax.axis_size(axis)
    ring = folded_ring(size)
    blocks = []
    for step in range(1, size):
        pairs = [(ring[i], ring[(i + step) % size]) for i in range(size)]
        blocks.append(lax.ppermute(block, axis, pairs))
    return blocks


def gather_by_mask(block, axis):
    size = lax.axis_size(axis)
    blocks = {0: block}
    for mask, source, bit in gather_plan(size):
        blocks[mask] = swap(blocks[source], axis, bit)
    return [blocks[m] for m in range(size)]


def load_kernel(count, *refs):
    sources, targets, arrived = refs[:count], refs[count:-1], refs[-1]
    copies = [
        pltpu.make_async_copy(source, target, arrived.at[i])
        for i, (source, target) in enumerate(zip(sources, targets))
    ]
    for copy in copies:
        copy.start()
    for copy in copies:
        copy.wait()


def load(*arrays):
    count = len(arrays)
    return pl.pallas_call(
        functools.partial(load_kernel, count),
        out_shape=tuple(pltpu.VMEM(a.shape, a.dtype) for a in arrays),
        in_specs=[HBM] * count,
        out_specs=(VMEM,) * count,
        scratch_shapes=[pltpu.SemaphoreType.DMA((count,))],
        compiler_params=PARAMS,
        name="load",
    )(*(pltpu.with_memory_space_constraint(a, pltpu.HBM) for a in arrays))


def project_kernel(count, *refs):
    strips, (gain, bias, w_query, w_keyval), outs = refs[:count], refs[count : count + 4], refs[count + 4 :]
    scale, shift = gain[...].reshape(1, -1), bias[...].reshape(1, -1)
    normed = []
    for strip in strips:
        values = strip[...].astype(jnp.float32)
        centred = values - jnp.mean(values, axis=-1, keepdims=True)
        variance = jnp.mean(centred * centred, axis=-1, keepdims=True)
        normed.append(
            (centred * lax.rsqrt(variance + 1e-05) * scale + shift).astype(jnp.bfloat16)
        )
    rows = jnp.concatenate(normed, axis=0)
    queries = lax.dot_general(
        rows, w_query[...], (((1,), (1,)), ((), ())), preferred_element_type=jnp.float32
    ).astype(jnp.bfloat16)
    keyval = jnp.dot(rows, w_keyval[...], preferred_element_type=jnp.float32).astype(jnp.bfloat16)
    middle = outs[0].shape[0]
    for index, part in enumerate((slice(0, middle), slice(middle, None))):
        chosen = queries[part]
        outs[2 * index][...] = jnp.concatenate([chosen, jnp.zeros_like(chosen)], axis=1)
        outs[2 * index + 1][...] = keyval[part]


def project(strips, params):
    rows = len(strips) // 2 * strips[0].shape[0]
    shape = pltpu.VMEM((rows, params[-1].shape[1]), jnp.bfloat16)
    return pl.pallas_call(
        functools.partial(project_kernel, len(strips)),
        out_shape=(shape,) * 4,
        in_specs=[VMEM] * (len(strips) + len(params)),
        out_specs=(VMEM,) * 4,
        compiler_params=PARAMS,
        name="project",
    )(*near(*strips, *params))


def attend_rows(head_size, tile, q_ref, key_refs, out_ref, scores):
    factor = math.log2(math.e) / math.sqrt(head_size)

    def one(rows):
        queries = q_ref[rows, :]
        start, row_max = 0, None
        for key in key_refs:
            size = key.shape[0]
            part = lax.dot_general(
                queries, key[...], (((1,), (1,)), ((), ())), preferred_element_type=jnp.float32
            )
            scores[:, start : start + size] = part
            top = jnp.max(part, axis=-1, keepdims=True)
            row_max = top if row_max is None else jnp.maximum(row_max, top)
            start += size
        start, total, weighted = 0, None, None
        for key in key_refs:
            size = key.shape[0]
            weights = jnp.exp2((scores[:, start : start + size] - row_max) * factor)
            part_sum = jnp.sum(weights, axis=-1, keepdims=True)
            part = jnp.dot(
                weights.astype(jnp.bfloat16), key[...], preferred_element_type=jnp.float32
            )
            total = part_sum if total is None else total + part_sum
            weighted = part if weighted is None else weighted + part
            start += size
        out_ref[rows, :] = (weighted[:, head_size:] / total).astype(jnp.bfloat16)

    steps = q_ref.shape[0] // tile
    if steps == 1:
        one(pl.ds(0, tile))
    else:

        def step(index, carry):
            one(pl.ds(pl.multiple_of(index * tile, tile), tile))
            return carry

        lax.fori_loop(0, steps, step, 0)


def score_tile(rows, keys):
    key_count = sum(k.shape[0] for k in keys)
    tile = rows
    while tile * key_count > SCORE_BUDGET and tile % 32 == 0:
        tile //= 2
    return tile, pltpu.VMEM((tile, key_count), jnp.float32)


def away_kernel(blocks, head_size, tile, q_ref, *refs):
    attend_rows(head_size, tile, q_ref, refs[:blocks], *refs[blocks:])


def attend_away(queries, keys, head_size):
    rows = queries.shape[0]
    tile, scores = score_tile(rows, keys)
    return pl.pallas_call(
        functools.partial(away_kernel, len(keys), head_size, tile),
        out_shape=pltpu.VMEM((rows, head_size), jnp.bfloat16),
        in_specs=[VMEM] * (1 + len(keys)),
        out_specs=VMEM,
        scratch_shapes=[scores],
        compiler_params=PARAMS,
        name="attend_away",
    )(*near(queries, *keys))


def home_kernel(blocks, head_size, tile, col_ref, q_ref, *refs):
    keys, (out_ref, fresh_out, scores, fresh, sent) = refs[:blocks], refs[blocks:]
    rows, count, width, lanes = fresh.shape
    each = rows * width
    for mask in range(count):
        strip = jnp.bitwise_xor(col_ref[0], mask)
        half, at = divmod(mask * each, keys[0].shape[0])
        fresh[:, strip] = keys[half][at : at + each, :].reshape(rows, width, lanes)
    copy = pltpu.make_async_copy(fresh, fresh_out, sent)
    copy.start()

    @pl.when(col_ref[0] >= 0)
    def _():
        attend_rows(head_size, tile, q_ref, keys, out_ref, scores)

    copy.wait()


def attend_home(col, queries, keys, head_size, fresh_shape):
    rows = queries.shape[0]
    tile, scores = score_tile(rows, keys)
    return pl.pallas_call(
        functools.partial(home_kernel, len(keys), head_size, tile),
        out_shape=(
            pltpu.VMEM((rows, head_size), jnp.bfloat16),
            jax.ShapeDtypeStruct(fresh_shape, jnp.bfloat16),
        ),
        in_specs=[SMEM] + [VMEM] * (1 + len(keys)),
        out_specs=(VMEM, HBM),
        scratch_shapes=[
            scores,
            pltpu.VMEM(fresh_shape, jnp.bfloat16),
            pltpu.SemaphoreType.DMA,
        ],
        compiler_params=PARAMS,
        name="attend_home",
    )(col, *near(queries, *keys))


def head_rows(col_ref, mask, w_ref, head_size):
    head = jnp.bitwise_xor(col_ref[0], mask)
    return w_ref[pl.ds(pl.multiple_of(head * head_size, head_size), head_size), :]


def begin_kernel(masks, col_ref, home, *refs):
    *parts, w_ref, bias, hidden, out_ref = refs
    head_size = home.shape[1]
    total = bias[...].reshape(1, -1) + hidden[...].astype(jnp.float32)
    for mask, part in zip((0, *masks), (home[: hidden.shape[0], :], *(p[...] for p in parts))):
        total = total + jnp.dot(
            part, head_rows(col_ref, mask, w_ref, head_size), preferred_element_type=jnp.float32
        )
    out_ref[...] = total


def begin(col, home, parts, w_out, bias, hidden):
    return pl.pallas_call(
        functools.partial(begin_kernel, tuple(parts)),
        out_shape=pltpu.VMEM(hidden.shape, jnp.float32),
        in_specs=[SMEM] + [VMEM] * (4 + len(parts)),
        out_specs=VMEM,
        compiler_params=PARAMS,
        name="begin",
    )(col, *near(home, *parts.values(), w_out, bias, hidden))


def finish_kernel(mask, col_ref, base, part, w_ref, out_ref, ready, sent):
    rows = head_rows(col_ref, mask, w_ref, part.shape[1])
    values = part[...]
    channels = base.shape[1]
    step = channels // 2 if channels % 256 == 0 else channels
    copies = []
    for index, start in enumerate(range(0, channels, step)):
        columns = slice(start, start + step)
        product = jnp.dot(values, rows[:, columns], preferred_element_type=jnp.float32)
        ready[:, columns] = (base[:, columns] + product).astype(jnp.bfloat16)
        copy = pltpu.make_async_copy(ready.at[:, columns], out_ref.at[:, columns], sent.at[index])
        copy.start()
        copies.append(copy)
    for copy in copies:
        copy.wait()


def finish(col, base, mask, part, w_out):
    return pl.pallas_call(
        functools.partial(finish_kernel, mask),
        out_shape=jax.ShapeDtypeStruct(base.shape, jnp.bfloat16),
        in_specs=[SMEM] + [VMEM] * 3,
        out_specs=HBM,
        scratch_shapes=[pltpu.VMEM(base.shape, jnp.bfloat16), pltpu.SemaphoreType.DMA((2,))],
        compiler_params=PARAMS,
        name="finish",
    )(col, *near(base, part, w_out))


def shards(hidden, ln_gain, ln_bias, w_query, w_keyval, stale_keyval, w_out, out_bias):
    band_rows, strip_cols, channels = hidden.shape
    head_size = w_query.shape[1]
    size = lax.axis_size("cols")
    half = size // 2
    each = band_rows * strip_cols
    own = hidden.reshape(each, channels)
    col = lax.axis_index("cols").astype(jnp.int32).reshape(1)
    strips = gather_by_mask(own, "cols")
    stale = gather_bands(stale_keyval.reshape(-1, 2 * head_size), "rows")
    near_own, near_out, near_bias, *params = load(
        own, w_out, out_bias, ln_gain, ln_bias, w_query.T, w_keyval
    )
    q_home, kv_home, q_away, kv_away = project([near_own, *strips[1:]], params)
    keys = [kv_home, kv_away] + stale
    away = attend_away(q_away, keys, head_size)
    fresh_shape = (band_rows, size, strip_cols, 2 * head_size)
    home, fresh = attend_home(col, q_home, keys, head_size, fresh_shape)
    mine = {}
    for mask in range(size - 1, 0, -1):
        block = away if mask >= half else home
        at = (mask % half) * each
        mine[mask] = swap(block[at : at + each], "cols", mask)
    last = mine.pop(half)
    base = begin(col, home, mine, near_out, near_bias, near_own)
    output = finish(col, base, half, last, near_out)
    return (
        output.reshape(hidden.shape),
        fresh.reshape(band_rows, size * strip_cols, 1, 2 * head_size),
    )


def solution(mesh):
    return jax.shard_map(
        shards,
        mesh=mesh,
        in_specs=(
            P(("groups", "rows"), "cols", None),
            P(),
            P(),
            P(None, "cols"),
            P(None, "cols"),
            P(("groups", "rows"), None, "cols", None),
            P(),
            P(),
        ),
        out_specs=(P(("groups", "rows"), "cols", None), P(("groups", "rows"), None, "cols", None)),
        check_vma=False,
    )
```

```python
import functools
import math

import jax
import jax.numpy as jnp
from jax import lax
from jax.experimental import pallas as pl
from jax.experimental.pallas import tpu as pltpu
from jax.sharding import PartitionSpec as P


SCORE_BUDGET = 1 << 17
VMEM = pl.BlockSpec(memory_space=pltpu.VMEM)
PARAMS = pltpu.CompilerParams(vmem_limit_bytes=24 << 20)
HBM = pl.BlockSpec(memory_space=pltpu.HBM)
SMEM = pl.BlockSpec(memory_space=pltpu.SMEM)


def near(*arrays):
    return [pltpu.with_memory_space_constraint(a, pltpu.VMEM) for a in arrays]


def swap(block, axis, mask):
    size = lax.axis_size(axis)
    return lax.ppermute(block, axis, [(i, i ^ mask) for i in range(size)])


def gather_plan(size):
    plan = []
    for mask in range(1, size):
        low = mask & -mask
        plan.append((mask, mask - low, low))
    return sorted(plan, key=lambda step: (bin(step[0]).count("1"), -step[2]))


def folded_ring(size):
    return [0, *range(1, size, 2), *reversed(range(2, size, 2))]


def gather_bands(block, axis):
    size = lax.axis_size(axis)
    ring = folded_ring(size)
    blocks = []
    for step in range(1, size):
        pairs = [(ring[i], ring[(i + step) % size]) for i in range(size)]
        blocks.append(lax.ppermute(block, axis, pairs))
    return blocks


def gather_by_mask(block, axis):
    size = lax.axis_size(axis)
    blocks = {0: block}
    for mask, source, bit in gather_plan(size):
        blocks[mask] = swap(blocks[source], axis, bit)
    return [blocks[m] for m in range(size)]


def load_kernel(count, *refs):
    sources, targets, arrived = refs[:count], refs[count:-1], refs[-1]
    copies = [
        pltpu.make_async_copy(source, target, arrived.at[i])
        for i, (source, target) in enumerate(zip(sources, targets))
    ]
    for copy in copies:
        copy.start()
    for copy in copies:
        copy.wait()


def load(*arrays):
    count = len(arrays)
    return pl.pallas_call(
        functools.partial(load_kernel, count),
        out_shape=tuple(pltpu.VMEM(a.shape, a.dtype) for a in arrays),
        in_specs=[HBM] * count,
        out_specs=(VMEM,) * count,
        scratch_shapes=[pltpu.SemaphoreType.DMA((count,))],
        compiler_params=PARAMS,
        name="load",
    )(*(pltpu.with_memory_space_constraint(a, pltpu.HBM) for a in arrays))


def project_kernel(count, *refs):
    strips, (gain, bias, w_query, w_keyval), outs = refs[:count], refs[count : count + 4], refs[count + 4 :]
    scale, shift = gain[...].reshape(1, -1), bias[...].reshape(1, -1)
    normed = []
    for strip in strips:
        values = strip[...].astype(jnp.float32)
        centred = values - jnp.mean(values, axis=-1, keepdims=True)
        variance = jnp.mean(centred * centred, axis=-1, keepdims=True)
        normed.append(
            (centred * lax.rsqrt(variance + 1e-05) * scale + shift).astype(jnp.bfloat16)
        )
    rows = jnp.concatenate(normed, axis=0)
    queries = lax.dot_general(
        rows, w_query[...], (((1,), (1,)), ((), ())), preferred_element_type=jnp.float32
    ).astype(jnp.bfloat16)
    keyval = jnp.dot(rows, w_keyval[...], preferred_element_type=jnp.float32).astype(jnp.bfloat16)
    middle = outs[0].shape[0]
    for index, part in enumerate((slice(0, middle), slice(middle, None))):
        chosen = queries[part]
        outs[2 * index][...] = jnp.concatenate([chosen, jnp.zeros_like(chosen)], axis=1)
        outs[2 * index + 1][...] = keyval[part]


def project(strips, params):
    rows = len(strips) // 2 * strips[0].shape[0]
    shape = pltpu.VMEM((rows, params[-1].shape[1]), jnp.bfloat16)
    return pl.pallas_call(
        functools.partial(project_kernel, len(strips)),
        out_shape=(shape,) * 4,
        in_specs=[VMEM] * (len(strips) + len(params)),
        out_specs=(VMEM,) * 4,
        compiler_params=PARAMS,
        name="project",
    )(*near(*strips, *params))


def attend_rows(head_size, tile, q_ref, key_refs, out_ref, scores):
    factor = math.log2(math.e) / math.sqrt(head_size)

    def one(rows):
        queries = q_ref[rows, :]
        start, row_max = 0, None
        for key in key_refs:
            size = key.shape[0]
            part = lax.dot_general(
                queries, key[...], (((1,), (1,)), ((), ())), preferred_element_type=jnp.float32
            )
            scores[:, start : start + size] = part
            top = jnp.max(part, axis=-1, keepdims=True)
            row_max = top if row_max is None else jnp.maximum(row_max, top)
            start += size
        start, total, weighted = 0, None, None
        for key in key_refs:
            size = key.shape[0]
            weights = jnp.exp2((scores[:, start : start + size] - row_max) * factor)
            part_sum = jnp.sum(weights, axis=-1, keepdims=True)
            part = jnp.dot(
                weights.astype(jnp.bfloat16), key[...], preferred_element_type=jnp.float32
            )
            total = part_sum if total is None else total + part_sum
            weighted = part if weighted is None else weighted + part
            start += size
        skipped = weighted.shape[1] - out_ref.shape[1]
        out_ref[rows, :] = (weighted[:, skipped:] / total).astype(jnp.bfloat16)

    steps = q_ref.shape[0] // tile
    if steps == 1:
        one(pl.ds(0, tile))
    else:

        def step(index, carry):
            one(pl.ds(pl.multiple_of(index * tile, tile), tile))
            return carry

        lax.fori_loop(0, steps, step, 0)


def score_tile(rows, keys):
    key_count = sum(k.shape[0] for k in keys)
    tile = rows
    while tile * key_count > SCORE_BUDGET and tile % 32 == 0:
        tile //= 2
    return tile, pltpu.VMEM((tile, key_count), jnp.float32)


def away_kernel(blocks, head_size, tile, q_ref, *refs):
    *packed, whole, scores = refs[blocks:]
    attend_rows(head_size, tile, q_ref, refs[:blocks], whole, scores)
    for index, out_ref in enumerate(packed):
        rows = out_ref.shape[0]
        start = 2 * rows * index
        out_ref[...] = jnp.concatenate(
            [
                whole[start : start + rows, head_size:],
                whole[start + rows : start + 2 * rows, head_size:],
            ],
            axis=1,
        )


def product_of(part, weights):
    head_size = weights.shape[0]
    if part.shape[1] != head_size:
        lane = lax.broadcasted_iota(jnp.int32, part.shape, 1)
        zeros = jnp.zeros_like(part)
        part = jnp.concatenate(
            [jnp.where(lane < head_size, part, zeros), jnp.where(lane < head_size, zeros, part)],
            axis=0,
        )
        weights = jnp.concatenate([weights, weights], axis=0)
    return jnp.dot(part, weights, preferred_element_type=jnp.float32)


def attend_away(queries, keys, head_size, each):
    rows = queries.shape[0]
    tile, scores = score_tile(rows, keys)
    count = rows // each
    return pl.pallas_call(
        functools.partial(away_kernel, len(keys), head_size, tile),
        out_shape=(pltpu.VMEM((each // 2, 2 * head_size), jnp.bfloat16),) * count,
        in_specs=[VMEM] * (1 + len(keys)),
        out_specs=(VMEM,) * count,
        scratch_shapes=[pltpu.VMEM(queries.shape, jnp.bfloat16), scores],
        compiler_params=PARAMS,
        name="attend_away",
    )(*near(queries, *keys))


def home_kernel(blocks, head_size, tile, col_ref, q_ref, *refs):
    keys, (out_ref, fresh_out, scores, fresh, sent) = refs[:blocks], refs[blocks:]
    rows, count, width, lanes = fresh.shape
    each = rows * width
    for mask in range(count):
        strip = jnp.bitwise_xor(col_ref[0], mask)
        half, at = divmod(mask * each, keys[0].shape[0])
        fresh[:, strip] = keys[half][at : at + each, :].reshape(rows, width, lanes)
    copy = pltpu.make_async_copy(fresh, fresh_out, sent)
    copy.start()

    @pl.when(col_ref[0] >= 0)
    def _():
        attend_rows(head_size, tile, q_ref, keys, out_ref, scores)

    copy.wait()


def attend_home(col, queries, keys, head_size, fresh_shape):
    rows = queries.shape[0]
    tile, scores = score_tile(rows, keys)
    return pl.pallas_call(
        functools.partial(home_kernel, len(keys), head_size, tile),
        out_shape=(
            pltpu.VMEM((rows, head_size), jnp.bfloat16),
            jax.ShapeDtypeStruct(fresh_shape, jnp.bfloat16),
        ),
        in_specs=[SMEM] + [VMEM] * (1 + len(keys)),
        out_specs=(VMEM, HBM),
        scratch_shapes=[
            scores,
            pltpu.VMEM(fresh_shape, jnp.bfloat16),
            pltpu.SemaphoreType.DMA,
        ],
        compiler_params=PARAMS,
        name="attend_home",
    )(col, *near(queries, *keys))


def head_rows(col_ref, mask, w_ref, head_size):
    head = jnp.bitwise_xor(col_ref[0], mask)
    return w_ref[pl.ds(pl.multiple_of(head * head_size, head_size), head_size), :]


def begin_kernel(masks, col_ref, home, *refs):
    *parts, w_ref, bias, hidden, out_ref = refs
    head_size = home.shape[1]
    total = bias[...].reshape(1, -1) + hidden[...].astype(jnp.float32)
    for mask, part in zip((0, *masks), (home[: hidden.shape[0], :], *(p[...] for p in parts))):
        total = total + product_of(part, head_rows(col_ref, mask, w_ref, head_size))
    out_ref[...] = total


def begin(col, home, parts, w_out, bias, hidden):
    return pl.pallas_call(
        functools.partial(begin_kernel, tuple(parts)),
        out_shape=pltpu.VMEM(hidden.shape, jnp.float32),
        in_specs=[SMEM] + [VMEM] * (4 + len(parts)),
        out_specs=VMEM,
        compiler_params=PARAMS,
        name="begin",
    )(col, *near(home, *parts.values(), w_out, bias, hidden))


def finish_kernel(mask, col_ref, base, part, w_ref, out_ref, ready, sent):
    head_size = part.shape[0] * part.shape[1] // base.shape[0]
    rows = head_rows(col_ref, mask, w_ref, head_size)
    values = part[...]
    channels = base.shape[1]
    step = channels // 2 if channels % 256 == 0 else channels
    copies = []
    for index, start in enumerate(range(0, channels, step)):
        columns = slice(start, start + step)
        product = product_of(values, rows[:, columns])
        ready[:, columns] = (base[:, columns] + product).astype(jnp.bfloat16)
        copy = pltpu.make_async_copy(ready.at[:, columns], out_ref.at[:, columns], sent.at[index])
        copy.start()
        copies.append(copy)
    for copy in copies:
        copy.wait()


def finish(col, base, mask, part, w_out):
    return pl.pallas_call(
        functools.partial(finish_kernel, mask),
        out_shape=jax.ShapeDtypeStruct(base.shape, jnp.bfloat16),
        in_specs=[SMEM] + [VMEM] * 3,
        out_specs=HBM,
        scratch_shapes=[pltpu.VMEM(base.shape, jnp.bfloat16), pltpu.SemaphoreType.DMA((2,))],
        compiler_params=PARAMS,
        name="finish",
    )(col, *near(base, part, w_out))


def shards(hidden, ln_gain, ln_bias, w_query, w_keyval, stale_keyval, w_out, out_bias):
    band_rows, strip_cols, channels = hidden.shape
    head_size = w_query.shape[1]
    size = lax.axis_size("cols")
    half = size // 2
    each = band_rows * strip_cols
    own = hidden.reshape(each, channels)
    col = lax.axis_index("cols").astype(jnp.int32).reshape(1)
    strips = gather_by_mask(own, "cols")
    stale = gather_bands(stale_keyval.reshape(-1, 2 * head_size), "rows")
    near_own, near_out, near_bias, *params = load(
        own, w_out, out_bias, ln_gain, ln_bias, w_query.T, w_keyval
    )
    q_home, kv_home, q_away, kv_away = project([near_own, *strips[1:]], params)
    keys = [kv_home, kv_away] + stale
    away = attend_away(q_away, keys, head_size, each)
    fresh_shape = (band_rows, size, strip_cols, 2 * head_size)
    home, fresh = attend_home(col, q_home, keys, head_size, fresh_shape)
    mine = {}
    for mask in range(size - 1, 0, -1):
        at = (mask % half) * each
        block = away[mask - half] if mask >= half else home[at : at + each]
        mine[mask] = swap(block, "cols", mask)
    last = mine.pop(half)
    base = begin(col, home, mine, near_out, near_bias, near_own)
    output = finish(col, base, half, last, near_out)
    return (
        output.reshape(hidden.shape),
        fresh.reshape(band_rows, size * strip_cols, 1, 2 * head_size),
    )


def solution(mesh):
    return jax.shard_map(
        shards,
        mesh=mesh,
        in_specs=(
            P(("groups", "rows"), "cols", None),
            P(),
            P(),
            P(None, "cols"),
            P(None, "cols"),
            P(("groups", "rows"), None, "cols", None),
            P(),
            P(),
        ),
        out_specs=(P(("groups", "rows"), "cols", None), P(("groups", "rows"), None, "cols", None)),
        check_vma=False,
    )
```

```python
import functools
import math

import jax
import jax.numpy as jnp
from jax import lax
from jax.experimental import pallas as pl
from jax.experimental.pallas import tpu as pltpu
from jax.sharding import PartitionSpec as P


SCORE_BUDGET = 1 << 17
VMEM = pl.BlockSpec(memory_space=pltpu.VMEM)
PARAMS = pltpu.CompilerParams(vmem_limit_bytes=24 << 20)
HBM = pl.BlockSpec(memory_space=pltpu.HBM)
SMEM = pl.BlockSpec(memory_space=pltpu.SMEM)


def near(*arrays):
    return [pltpu.with_memory_space_constraint(a, pltpu.VMEM) for a in arrays]


def swap(block, axis, mask):
    size = lax.axis_size(axis)
    return lax.ppermute(block, axis, [(i, i ^ mask) for i in range(size)])


def gather_plan(size):
    plan = []
    for mask in range(1, size):
        low = mask & -mask
        plan.append((mask, mask - low, low))
    return sorted(plan, key=lambda step: (bin(step[0]).count("1"), -step[2]))


def folded_ring(size):
    return [0, *range(1, size, 2), *reversed(range(2, size, 2))]


def gather_bands(block, axis):
    size = lax.axis_size(axis)
    ring = folded_ring(size)
    blocks = []
    for step in range(1, size):
        pairs = [(ring[i], ring[(i + step) % size]) for i in range(size)]
        blocks.append(lax.ppermute(block, axis, pairs))
    return blocks


def gather_by_mask(block, axis):
    size = lax.axis_size(axis)
    blocks = {0: block}
    for mask, source, bit in gather_plan(size):
        blocks[mask] = swap(blocks[source], axis, bit)
    return [blocks[m] for m in range(size)]


def load_kernel(count, *refs):
    sources, targets, arrived = refs[:count], refs[count:-1], refs[-1]
    copies = [
        pltpu.make_async_copy(source, target, arrived.at[i])
        for i, (source, target) in enumerate(zip(sources, targets))
    ]
    for copy in copies:
        copy.start()
    for copy in copies:
        copy.wait()


def load(*arrays):
    count = len(arrays)
    return pl.pallas_call(
        functools.partial(load_kernel, count),
        out_shape=tuple(pltpu.VMEM(a.shape, a.dtype) for a in arrays),
        in_specs=[HBM] * count,
        out_specs=(VMEM,) * count,
        scratch_shapes=[pltpu.SemaphoreType.DMA((count,))],
        compiler_params=PARAMS,
        name="load",
    )(*(pltpu.with_memory_space_constraint(a, pltpu.HBM) for a in arrays))


def project_kernel(count, *refs):
    strips, (gain, bias, w_query, w_keyval), outs = refs[:count], refs[count : count + 4], refs[count + 4 :]
    scale, shift = gain[...].reshape(1, -1), bias[...].reshape(1, -1)
    normed = []
    for strip in strips:
        values = strip[...].astype(jnp.float32)
        centred = values - jnp.mean(values, axis=-1, keepdims=True)
        variance = jnp.mean(centred * centred, axis=-1, keepdims=True)
        normed.append(
            (centred * lax.rsqrt(variance + 1e-05) * scale + shift).astype(jnp.bfloat16)
        )
    rows = jnp.concatenate(normed, axis=0)
    queries = lax.dot_general(
        rows, w_query[...], (((1,), (1,)), ((), ())), preferred_element_type=jnp.float32
    ).astype(jnp.bfloat16)
    keyval = jnp.dot(rows, w_keyval[...], preferred_element_type=jnp.float32).astype(jnp.bfloat16)
    middle = outs[0].shape[0]
    for index, part in enumerate((slice(0, middle), slice(middle, None))):
        chosen = queries[part]
        outs[2 * index][...] = jnp.concatenate([chosen, jnp.zeros_like(chosen)], axis=1)
        outs[2 * index + 1][...] = keyval[part]


def project(strips, params):
    rows = len(strips) // 2 * strips[0].shape[0]
    shape = pltpu.VMEM((rows, params[-1].shape[1]), jnp.bfloat16)
    return pl.pallas_call(
        functools.partial(project_kernel, len(strips)),
        out_shape=(shape,) * 4,
        in_specs=[VMEM] * (len(strips) + len(params)),
        out_specs=(VMEM,) * 4,
        compiler_params=PARAMS,
        name="project",
    )(*near(*strips, *params))


def attend_rows(head_size, tile, q_ref, key_refs, out_ref, scores):
    factor = math.log2(math.e) / math.sqrt(head_size)

    def one(rows):
        queries = q_ref[rows, :]
        start, row_max = 0, None
        for key in key_refs:
            size = key.shape[0]
            part = lax.dot_general(
                queries, key[...], (((1,), (1,)), ((), ())), preferred_element_type=jnp.float32
            )
            scores[:, start : start + size] = part
            top = jnp.max(part, axis=-1, keepdims=True)
            row_max = top if row_max is None else jnp.maximum(row_max, top)
            start += size
        start, total, weighted = 0, None, None
        for key in key_refs:
            size = key.shape[0]
            weights = jnp.exp2((scores[:, start : start + size] - row_max) * factor)
            part_sum = jnp.sum(weights, axis=-1, keepdims=True)
            part = jnp.dot(
                weights.astype(jnp.bfloat16), key[...], preferred_element_type=jnp.float32
            )
            total = part_sum if total is None else total + part_sum
            weighted = part if weighted is None else weighted + part
            start += size
        skipped = weighted.shape[1] - out_ref.shape[1]
        out_ref[rows, :] = (weighted[:, skipped:] / total).astype(jnp.bfloat16)

    steps = q_ref.shape[0] // tile
    if steps == 1:
        one(pl.ds(0, tile))
    else:

        def step(index, carry):
            one(pl.ds(pl.multiple_of(index * tile, tile), tile))
            return carry

        lax.fori_loop(0, steps, step, 0)


def score_tile(rows, keys):
    key_count = sum(k.shape[0] for k in keys)
    tile = rows
    while tile * key_count > SCORE_BUDGET and tile % 32 == 0:
        tile //= 2
    return tile, pltpu.VMEM((tile, key_count), jnp.float32)


def away_kernel(blocks, head_size, tile, q_ref, *refs):
    *packed, whole, scores = refs[blocks:]
    attend_rows(head_size, tile, q_ref, refs[:blocks], whole, scores)
    pack(whole, packed, head_size)


def pack(whole, packed, head_size):
    for index, out_ref in enumerate(packed):
        rows = out_ref.shape[0]
        start = 2 * rows * index
        out_ref[...] = jnp.concatenate(
            [
                whole[start : start + rows, head_size:],
                whole[start + rows : start + 2 * rows, head_size:],
            ],
            axis=1,
        )


def product_of(part, weights):
    head_size = weights.shape[0]
    if part.shape[1] != head_size:
        lane = lax.broadcasted_iota(jnp.int32, part.shape, 1)
        zeros = jnp.zeros_like(part)
        part = jnp.concatenate(
            [jnp.where(lane < head_size, part, zeros), jnp.where(lane < head_size, zeros, part)],
            axis=0,
        )
        weights = jnp.concatenate([weights, weights], axis=0)
    return jnp.dot(part, weights, preferred_element_type=jnp.float32)


def attend_away(queries, keys, head_size, each):
    rows = queries.shape[0]
    tile, scores = score_tile(rows, keys)
    count = rows // each
    return pl.pallas_call(
        functools.partial(away_kernel, len(keys), head_size, tile),
        out_shape=(pltpu.VMEM((each // 2, 2 * head_size), jnp.bfloat16),) * count,
        in_specs=[VMEM] * (1 + len(keys)),
        out_specs=(VMEM,) * count,
        scratch_shapes=[pltpu.VMEM(queries.shape, jnp.bfloat16), scores],
        compiler_params=PARAMS,
        name="attend_away",
    )(*near(queries, *keys))


def home_kernel(blocks, head_size, tile, col_ref, q_ref, *refs):
    keys, (*packed, fresh_out, whole, scores, fresh, sent) = refs[:blocks], refs[blocks:]
    rows, count, width, lanes = fresh.shape
    each = rows * width
    for mask in range(count):
        strip = jnp.bitwise_xor(col_ref[0], mask)
        half, at = divmod(mask * each, keys[0].shape[0])
        fresh[:, strip] = keys[half][at : at + each, :].reshape(rows, width, lanes)
    copy = pltpu.make_async_copy(fresh, fresh_out, sent)
    copy.start()

    @pl.when(col_ref[0] >= 0)
    def _():
        attend_rows(head_size, tile, q_ref, keys, whole, scores)
        pack(whole, packed, head_size)

    copy.wait()


def attend_home(col, queries, keys, head_size, fresh_shape):
    rows = queries.shape[0]
    tile, scores = score_tile(rows, keys)
    each = fresh_shape[0] * fresh_shape[2]
    count = rows // each
    return pl.pallas_call(
        functools.partial(home_kernel, len(keys), head_size, tile),
        out_shape=(
            *((pltpu.VMEM((each // 2, 2 * head_size), jnp.bfloat16),) * count),
            jax.ShapeDtypeStruct(fresh_shape, jnp.bfloat16),
        ),
        in_specs=[SMEM] + [VMEM] * (1 + len(keys)),
        out_specs=(VMEM,) * count + (HBM,),
        scratch_shapes=[
            pltpu.VMEM(queries.shape, jnp.bfloat16),
            scores,
            pltpu.VMEM(fresh_shape, jnp.bfloat16),
            pltpu.SemaphoreType.DMA,
        ],
        compiler_params=PARAMS,
        name="attend_home",
    )(col, *near(queries, *keys))


def head_rows(col_ref, mask, w_ref, head_size):
    head = jnp.bitwise_xor(col_ref[0], mask)
    return w_ref[pl.ds(pl.multiple_of(head * head_size, head_size), head_size), :]


def begin_kernel(masks, col_ref, home, *refs):
    *parts, w_ref, bias, hidden, out_ref = refs
    head_size = home.shape[0] * home.shape[1] // hidden.shape[0]
    total = bias[...].reshape(1, -1) + hidden[...].astype(jnp.float32)
    for mask, part in zip((0, *masks), (home[...], *(p[...] for p in parts))):
        total = total + product_of(part, head_rows(col_ref, mask, w_ref, head_size))
    out_ref[...] = total


def begin(col, home, parts, w_out, bias, hidden):
    return pl.pallas_call(
        functools.partial(begin_kernel, tuple(parts)),
        out_shape=pltpu.VMEM(hidden.shape, jnp.float32),
        in_specs=[SMEM] + [VMEM] * (4 + len(parts)),
        out_specs=VMEM,
        compiler_params=PARAMS,
        name="begin",
    )(col, *near(home, *parts.values(), w_out, bias, hidden))


def finish_kernel(mask, col_ref, base, part, w_ref, out_ref, ready, sent):
    head_size = part.shape[0] * part.shape[1] // base.shape[0]
    rows = head_rows(col_ref, mask, w_ref, head_size)
    values = part[...]
    channels = base.shape[1]
    step = channels // 2 if channels % 256 == 0 else channels
    copies = []
    for index, start in enumerate(range(0, channels, step)):
        columns = slice(start, start + step)
        product = product_of(values, rows[:, columns])
        ready[:, columns] = (base[:, columns] + product).astype(jnp.bfloat16)
        copy = pltpu.make_async_copy(ready.at[:, columns], out_ref.at[:, columns], sent.at[index])
        copy.start()
        copies.append(copy)
    for copy in copies:
        copy.wait()


def finish(col, base, mask, part, w_out):
    return pl.pallas_call(
        functools.partial(finish_kernel, mask),
        out_shape=jax.ShapeDtypeStruct(base.shape, jnp.bfloat16),
        in_specs=[SMEM] + [VMEM] * 3,
        out_specs=HBM,
        scratch_shapes=[pltpu.VMEM(base.shape, jnp.bfloat16), pltpu.SemaphoreType.DMA((2,))],
        compiler_params=PARAMS,
        name="finish",
    )(col, *near(base, part, w_out))


def shards(hidden, ln_gain, ln_bias, w_query, w_keyval, stale_keyval, w_out, out_bias):
    band_rows, strip_cols, channels = hidden.shape
    head_size = w_query.shape[1]
    size = lax.axis_size("cols")
    half = size // 2
    each = band_rows * strip_cols
    own = hidden.reshape(each, channels)
    col = lax.axis_index("cols").astype(jnp.int32).reshape(1)
    strips = gather_by_mask(own, "cols")
    stale = gather_bands(stale_keyval.reshape(-1, 2 * head_size), "rows")
    near_own, near_out, near_bias, *params = load(
        own, w_out, out_bias, ln_gain, ln_bias, w_query.T, w_keyval
    )
    q_home, kv_home, q_away, kv_away = project([near_own, *strips[1:]], params)
    keys = [kv_home, kv_away] + stale
    away = attend_away(q_away, keys, head_size, each)
    fresh_shape = (band_rows, size, strip_cols, 2 * head_size)
    *home, fresh = attend_home(col, q_home, keys, head_size, fresh_shape)
    mine = {}
    for mask in range(size - 1, 0, -1):
        block = away[mask - half] if mask >= half else home[mask]
        mine[mask] = swap(block, "cols", mask)
    last = mine.pop(half)
    base = begin(col, home[0], mine, near_out, near_bias, near_own)
    output = finish(col, base, half, last, near_out)
    return (
        output.reshape(hidden.shape),
        fresh.reshape(band_rows, size * strip_cols, 1, 2 * head_size),
    )


def solution(mesh):
    return jax.shard_map(
        shards,
        mesh=mesh,
        in_specs=(
            P(("groups", "rows"), "cols", None),
            P(),
            P(),
            P(None, "cols"),
            P(None, "cols"),
            P(("groups", "rows"), None, "cols", None),
            P(),
            P(),
        ),
        out_specs=(P(("groups", "rows"), "cols", None), P(("groups", "rows"), None, "cols", None)),
        check_vma=False,
    )
```
